32 devices in a mesh: seg: 4 (over z), rank: 8 (over y, x, core).
Axes of the slice: x: 2, y: 2, z: 4, core: 2. Of those that a mesh axis runs over, the one named last changes fastest.
Arguments:
- children: float32 [20, 35, 65536], P(None, None, ('seg', 'rank')), may hold values from -6 to 6
- pair_order: int32 [32, 2048], P(('seg', 'rank')), may hold values from 0 to 2047, each once within a row
- rim_order: int32 [32, 256], P(('seg', 'rank')), may hold values from 0 to 255, each once within a row
- pair_type: int32 [32, 1024], P(('seg', 'rank')), may hold values from 0 to 2
- projection: float32 [3, 2, 35, 35], replicated, may hold values from -0.75 to 0.75
- new_owner: int32 [32, 1024], P(('seg', 'rank')), may hold values from 0 to 31, as said below
- new_slot: int32 [32, 1024], P(('seg', 'rank')), may hold values from 0 to 1023, as said below
Outputs:
- parents: float32 [20, 35, 32768], P(None, None, ('seg', 'rank'))
The draws below stay inside these ranges and needn't reach their ends.
Inputs may be any that keep to these rules, and one draw needn't show every extreme that they name: `pair_order`: each row is a permutation. `rim_order`: each row is a permutation. `new_owner`: A device of seg g and rank r sends its parents to itself, to other devices of seg g, and to rank r of seg g + 1 (segments counted around); at most 64 to each other device of its seg, exactly 64 to rank r + 1 of seg g (ranks counted around), exactly 64 to seg g + 1; every device receives exactly 1024 parents. The pairs (new_owner, new_slot) are distinct over all parents.
All inputs are finite; a program needn't handle non-finite values.
Results may differ from the reference program's by a relative error of at most 0.0003.
Values sent between devices are 32-bit elements; how exact they have to be, the bound alone decides.
A program may use at most 192 MiB of HBM per device.

```python
import jax
import jax.numpy as jnp
from jax import lax

FIELDS = 20
MODES = 35
TYPES = 3
CH_DEV = 2048
PAR_DEV = 1024
BORDER = 256
NEAR_CAP = 64
FAR_CAP = 64
CHILDREN = 65536
PARENTS = 32768
N_SEG = 4
N_RANK = 8


def routing(key):
    base = jax.random.fold_in(key, 11)
    key_weights, key_send, key_recv = jax.random.split(base, 3)
    device_count = N_SEG * N_RANK
    others = jax.random.randint(key_weights, (N_RANK - 2,), NEAR_CAP // 2, NEAR_CAP + 1).astype(jnp.int32)
    nearby = jnp.concatenate([jnp.array([NEAR_CAP], jnp.int32), others])
    staying = PAR_DEV - FAR_CAP - jnp.sum(nearby)
    weights = jnp.concatenate([staying[None].astype(jnp.int32), nearby, jnp.array([FAR_CAP], jnp.int32)])
    ends = jnp.cumsum(weights)
    send_keys = jax.random.split(key_send, device_count)
    position = jax.vmap(lambda k: jax.random.permutation(k, PAR_DEV))(send_keys).astype(jnp.int32)
    category = jnp.sum((position[:, :, None] >= ends[None, None, :]).astype(jnp.int32), axis=2)
    device = jnp.arange(device_count, dtype=jnp.int32)[:, None]
    seg_index = device // N_RANK
    rank_index = device % N_RANK
    distant = (category == N_RANK).astype(jnp.int32)
    offset = jnp.where(category == N_RANK, 0, category)
    owner_ids = (seg_index + distant) % N_SEG * N_RANK + (rank_index + offset) % N_RANK
    recv_keys = jax.random.split(key_recv, device_count)
    receiving = jax.vmap(lambda k: jax.random.permutation(k, PAR_DEV))(recv_keys).astype(jnp.int32)
    slot_ids = receiving[owner_ids, position]
    return (owner_ids.astype(jnp.int32), slot_ids.astype(jnp.int32))


def draw_new_owner(key, part):
    return routing(key)[0]


def draw_new_slot(key, part):
    return routing(key)[1]


def with_ends(result, own_key, least, largest):
    spot = [jax.random.randint(jax.random.fold_in(own_key, axis), (), 0, length) for axis, length in enumerate(result.shape)]
    main_axis = result.shape.index(max(result.shape))
    beside = spot[:main_axis] + [(spot[main_axis] + 1) % result.shape[main_axis]] + spot[main_axis + 1:]
    return result.at[tuple(spot)].set(least).at[tuple(beside)].set(largest)


def level_of(own_key, extent, pieces, low, top_value):
    gain = 1.0
    for axis_at, blocks in pieces:
        heights = jax.random.uniform(jax.random.fold_in(jax.random.fold_in(own_key, 6), axis_at), (blocks,), jnp.float32, low / len(pieces), top_value / len(pieces))
        gain = gain * jnp.repeat(jnp.exp(heights), extent[axis_at] // blocks).reshape((-1,) + (1,) * (len(extent) - 1 - axis_at))
    return gain


def bell_draw(stream_key, shape, deviation, limit, shards=(), held_as=jnp.bfloat16):
    level = level_of(stream_key, shape, shards, -0.22, 0.18) if shards else 1.0
    values = jax.random.normal(stream_key, shape, jnp.float32) * deviation * level
    return jnp.minimum(jnp.maximum(values, -limit), limit).astype(held_as)


def setup_inputs(seed: int = 0) -> dict:
    key_list = jax.random.split(jax.random.key(seed), 8)
    return {
        "children": bell_draw(key_list[0], (FIELDS, MODES, CHILDREN), 1.0, 6.0, ((2, 32),), jnp.float32),
        "pair_order": jax.vmap(lambda own: jax.random.permutation(own, CH_DEV))(jax.random.split(key_list[1], (N_SEG * N_RANK))).reshape((N_SEG * N_RANK, CH_DEV)).astype(jnp.int32),
        "rim_order": jax.vmap(lambda own: jax.random.permutation(own, BORDER))(jax.random.split(key_list[2], (N_SEG * N_RANK))).reshape((N_SEG * N_RANK, BORDER)).astype(jnp.int32),
        "pair_type": with_ends(jax.random.randint(key_list[3], (N_SEG * N_RANK, PAR_DEV), 0, TYPES), jax.random.fold_in(key_list[3], 1), 0, TYPES - 1).astype(jnp.int32),
        "projection": bell_draw(key_list[4], (TYPES, 2, MODES, MODES), (2 * MODES) ** -0.5, 0.75, (), jnp.float32),
        "new_owner": draw_new_owner(jax.random.fold_in(key_list[7], 71), 0),
        "new_slot": draw_new_slot(jax.random.fold_in(key_list[7], 71), 0),
    }


def project(projection, first_child, second_child, pair_kinds):
    field_count = first_child.shape[0]
    mode_count = projection.shape[2]
    kind_count = projection.shape[0]
    stacked_first = projection[:, 0].reshape(kind_count * mode_count, mode_count)
    stacked_second = projection[:, 1].reshape(kind_count * mode_count, mode_count)
    wide_first = jnp.broadcast_to(stacked_first[None], (field_count,) + stacked_first.shape)
    wide_second = jnp.broadcast_to(stacked_second[None], (field_count,) + stacked_second.shape)
    dims = (((2,), (1,)), ((0,), (0,)))
    total = lax.dot_general(wide_first, first_child, dims, precision=lax.Precision.HIGHEST, preferred_element_type=jnp.float32)
    total = total + lax.dot_general(wide_second, second_child, dims, precision=lax.Precision.HIGHEST, preferred_element_type=jnp.float32)
    total = total.reshape(field_count, kind_count, mode_count, first_child.shape[2])
    chosen = (pair_kinds[None, :] == jnp.arange(kind_count, dtype=jnp.int32)[:, None])
    return jnp.sum(jnp.where(chosen[None, :, None, :], total, 0.0), axis=1)


def reference(children, pair_order, rim_order, pair_type, projection, new_owner, new_slot):
    device_count = N_SEG * N_RANK
    blocks = children.reshape(FIELDS, MODES, device_count, CH_DEV)
    rim_blocks = jnp.roll(blocks[:, :, :, :BORDER], -1, axis=2)

    def per_device(device):
        own_block = lax.dynamic_index_in_dim(blocks, device, 2, keepdims=False)
        rim_block = lax.dynamic_index_in_dim(rim_blocks, device, 2, keepdims=False)
        rim_block = jnp.take(rim_block, rim_order[device], axis=2)
        extended = jnp.concatenate([own_block[:, :, BORDER:], rim_block], axis=2)
        pair_rows = pair_order[device].reshape(PAR_DEV, 2)
        first_child = jnp.take(extended, pair_rows[:, 0], axis=2)
        second_child = jnp.take(extended, pair_rows[:, 1], axis=2)
        return project(projection, first_child, second_child, pair_type[device])

    values = lax.map(per_device, jnp.arange(device_count, dtype=jnp.int32))
    target = (new_owner * PAR_DEV + new_slot).reshape(-1).astype(jnp.int32)
    parents_flat = jnp.moveaxis(values, 0, 2).reshape(FIELDS, MODES, PARENTS)
    source = jnp.zeros((PARENTS,), jnp.int32).at[target].set(jnp.arange(PARENTS, dtype=jnp.int32))
    return jnp.take(parents_flat, source, axis=2)
```

```python
import functools

import jax
import jax.numpy as jnp
from jax import lax
from jax.experimental import pallas as pl
from jax.experimental.pallas import tpu as pltpu
from jax.sharding import PartitionSpec as P

LANES = 128
SUB = 8
F32 = jnp.float32
BF16 = jnp.bfloat16
I32 = jnp.int32


def passed_along(x, axis, by):
    count = lax.axis_size(axis)
    return lax.ppermute(x, axis, [(i, (i + by) % count) for i in range(count)])


def row(i):
    return pl.ds(pl.multiple_of(i * SUB, SUB), SUB)


def split(x):
    high = x.astype(BF16)
    low = (x - high.astype(F32)).astype(BF16)
    return high, low


def column_of(line):
    return jnp.broadcast_to(line, (LANES, line.shape[1])).T


def make_kernel(
    n_rank,
    near_cap,
    far_cap,
    fields,
    modes,
    rim_len,
    kinds,
    children,
    rim,
    pair_s,
    rim_s,
    kind_v,
    owner_v,
    slot_v,
    where_v,
    weight,
    home_out,
    near_out,
    far_out,
    stage,
    ext,
    first,
    second,
    value,
    sorted_rows,
    target_v,
    target_s,
    sems,
):
    child_count = children.shape[2]
    parent_count = child_count // 2
    pitch = (modes + 7) // 8 * 8
    per_group = LANES // pitch
    groups = -(-fields // per_group)
    near_total = n_rank * near_cap
    kept = child_count - rim_len

    me = where_v[0:1, 0:1]
    owner = owner_v[...]
    slot = slot_v[...]
    my_seg = me // n_rank
    my_rank = me - my_seg * n_rank
    owner_seg = owner // n_rank
    owner_rank = owner - owner_seg * n_rank
    distant = owner_seg != my_seg
    staying = owner == me
    bin_of = jnp.where(distant, n_rank, jnp.where(staying, -1, owner_rank))
    bins = -(-(n_rank + 1) // 16) * 16
    hot = jnp.where(
        lax.broadcasted_iota(I32, (bins, parent_count), 0) == bin_of, 1.0, 0.0
    )
    ahead = jnp.where(
        lax.broadcasted_iota(I32, (parent_count, parent_count), 0)
        < lax.broadcasted_iota(I32, (parent_count, parent_count), 1),
        1.0,
        0.0,
    ).astype(BF16)
    counted = jnp.dot(hot.astype(BF16), ahead, preferred_element_type=F32)
    place = jnp.sum(counted * hot, axis=0, keepdims=True).astype(I32)
    target = jnp.where(staying, slot, parent_count + bin_of * near_cap + place)
    target_v[...] = jnp.broadcast_to(target, target_v.shape)
    to_scalar = pltpu.make_async_copy(target_v, target_s, sems.at[3])
    to_scalar.start()

    stage[...] = jnp.zeros_like(stage)
    for g in range(groups):
        for j in range(per_group):
            f = g * per_group + j
            if f < fields:
                stage[pitch * j : pitch * j + modes, 0:kept] = children[f, :, rim_len:]
                stage[pitch * j : pitch * j + modes, kept:] = rim[f]

        def turn(c, carry, g=g):
            block = stage[:, pl.ds(pl.multiple_of(c * LANES, LANES), LANES)]
            ext[pl.ds(c * LANES * SUB + g, LANES, stride=SUB), :] = block.T
            return carry

        lax.fori_loop(0, child_count // LANES, turn, 0, unroll=4)

    def border(e, carry):
        ext[row(child_count + e), :] = ext[row(kept + rim_s[0, e]), :]
        return carry

    lax.fori_loop(0, rim_len, border, 0, unroll=8)

    def pick(q, carry):
        a = pair_s[0, 2 * q]
        b = pair_s[0, 2 * q + 1]
        a = jnp.where(a >= kept, a + rim_len, a)
        b = jnp.where(b >= kept, b + rim_len, b)
        first[row(q), :] = ext[row(a), :]
        second[row(q), :] = ext[row(b), :]
        return carry

    lax.fori_loop(0, parent_count, pick, 0, unroll=8)

    w_high, w_low = split(weight[...])
    w_both = jnp.concatenate([w_high, w_low], axis=1)
    wide = kinds * LANES
    rows_at = min(256, parent_count)

    def project(b, carry):
        kind = jnp.concatenate(
            [
                column_of(kind_v[:, pl.ds(pl.multiple_of(b * rows_at + c * LANES, LANES), LANES)])
                for c in range(rows_at // LANES)
            ],
            axis=0,
        )
        slots = jnp.concatenate(
            [
                column_of(slot_v[:, pl.ds(pl.multiple_of(b * rows_at + c * LANES, LANES), LANES)])
                for c in range(rows_at // LANES)
            ],
            axis=0,
        )
        for g in range(groups):
            at = pl.ds(b * rows_at * SUB + g, rows_at, stride=SUB)
            pair = jnp.concatenate([first[at, :], second[at, :]], axis=1)
            high, low = split(pair)
            both = jnp.dot(high, w_both, preferred_element_type=F32)
            total = both[:, :wide] + both[:, wide:]
            total = total + jnp.dot(low, w_high, preferred_element_type=F32)
            chosen = total[:, :LANES]
            for t in range(1, kinds):
                chosen = jnp.where(kind == t, total[:, t * LANES : (t + 1) * LANES], chosen)
            value[at, :] = chosen
        value[pl.ds(b * rows_at * SUB + SUB - 1, rows_at, stride=SUB), :] = slots.astype(F32)
        return carry

    lax.fori_loop(0, parent_count // rows_at, project, 0)

    sorted_rows[parent_count * SUB : (parent_count + near_total) * SUB, :] = jnp.full(
        (near_total * SUB, LANES), float(parent_count), F32
    )
    to_scalar.wait()

    def place_row(q, carry):
        sorted_rows[row(target_s[0, q]), :] = value[row(q), :]
        return carry

    lax.fori_loop(0, parent_count, place_row, 0, unroll=8)
    far_at = (parent_count + near_total) * SUB
    copies = [
        pltpu.make_async_copy(
            sorted_rows.at[pl.ds(parent_count * SUB, near_total * SUB), :], near_out, sems.at[0]
        ),
        pltpu.make_async_copy(
            sorted_rows.at[pl.ds(far_at, far_cap * SUB), :], far_out, sems.at[1]
        ),
        pltpu.make_async_copy(
            sorted_rows.at[pl.ds(0, parent_count * SUB), :], home_out, sems.at[2]
        ),
    ]
    for copy in copies:
        copy.start()
    for copy in copies:
        copy.wait()


def land_kernel(fields, modes, home, near, far, out, rows, slot_v, slot_s, sems):
    parent_count = out.shape[2]
    near_total = near.shape[0] // SUB
    far_cap = far.shape[0] // SUB
    pitch = (modes + 7) // 8 * 8
    per_group = LANES // pitch
    groups = -(-fields // per_group)
    from_home = pltpu.make_async_copy(
        home, rows.at[pl.ds(0, parent_count * SUB), :], sems.at[0]
    )
    from_home.start()
    for c in range(near_total // LANES):
        tile = near[pl.ds(c * LANES * SUB + SUB - 1, LANES, stride=SUB), :].T
        slot_v[:, c * LANES : (c + 1) * LANES] = tile[0:SUB].astype(I32)
    far_slots = far[pl.ds(SUB - 1, far_cap, stride=SUB), :]
    far_slots = jnp.concatenate([far_slots] * (LANES // far_cap), axis=0).T
    slot_v[:, near_total : near_total + LANES] = far_slots[0:SUB].astype(I32)
    to_scalar = pltpu.make_async_copy(slot_v, slot_s, sems.at[1])
    to_scalar.start()
    from_home.wait()
    to_scalar.wait()

    def put_near(i, carry):
        rows[row(slot_s[0, i]), :] = near[row(i), :]
        return carry

    lax.fori_loop(0, near_total, put_near, 0, unroll=8)

    def put_far(i, carry):
        rows[row(slot_s[0, near_total + i]), :] = far[row(i), :]
        return carry

    lax.fori_loop(0, far_cap, put_far, 0, unroll=8)

    for g in range(groups):
        for c in range(parent_count // LANES):
            tile = rows[pl.ds(c * LANES * SUB + g, LANES, stride=SUB), :].T
            for j in range(per_group):
                f = g * per_group + j
                if f < fields:
                    out[f, :, c * LANES : (c + 1) * LANES] = tile[
                        pitch * j : pitch * j + modes
                    ]


def wide_weights(projection):
    kinds, _, modes, _ = projection.shape
    pitch = (modes + 7) // 8 * 8
    per_group = LANES // pitch
    small = jnp.pad(projection, ((0, 0), (0, 0), (0, pitch - modes), (0, pitch - modes)))
    small = jnp.transpose(small, (1, 3, 0, 2))
    tiled = jnp.tile(small, (1, per_group, 1, per_group))
    at = jnp.arange(per_group * pitch, dtype=I32) // pitch
    tiled = jnp.where((at[:, None] == at[None, :])[None, :, None, :], tiled, 0.0)
    left = LANES - per_group * pitch
    tiled = jnp.pad(tiled, ((0, 0), (0, left), (0, 0), (0, left)))
    return tiled.reshape(2 * LANES, kinds * LANES)


def per_device(children, pair_order, rim_order, pair_type, projection, new_owner, new_slot):
    fields, modes, child_count = children.shape
    rim_len = rim_order.shape[1]
    parent_count = child_count // 2
    kinds = projection.shape[0]
    n_rank = lax.axis_size("rank")
    near_cap = parent_count // (2 * n_rank)
    far_cap = parent_count // 16
    near_total = n_rank * near_cap
    rim = passed_along(children[:, :, :rim_len], ("seg", "rank"), -1)
    me = lax.axis_index("seg") * n_rank + lax.axis_index("rank")
    where = jnp.full((SUB, LANES), me, I32)
    weight = wide_weights(projection)
    vmem = pl.BlockSpec(memory_space=pltpu.VMEM)
    smem = pl.BlockSpec(memory_space=pltpu.SMEM)
    hbm = pl.BlockSpec(memory_space=pl.ANY)
    params = pltpu.CompilerParams(vmem_limit_bytes=56 * 1024 * 1024)
    home, near, far = pl.pallas_call(
        functools.partial(
            make_kernel, n_rank, near_cap, far_cap, fields, modes, rim_len, kinds
        ),
        out_shape=[
            jax.ShapeDtypeStruct((parent_count * SUB, LANES), F32),
            jax.ShapeDtypeStruct((near_total * SUB, LANES), F32),
            jax.ShapeDtypeStruct((far_cap * SUB, LANES), F32),
        ],
        in_specs=[vmem, vmem, smem, smem, vmem, vmem, vmem, vmem, vmem],
        out_specs=[hbm, hbm, hbm],
        scratch_shapes=[
            pltpu.VMEM((LANES, child_count), F32),
            pltpu.VMEM(((child_count + rim_len) * SUB, LANES), F32),
            pltpu.VMEM((parent_count * SUB, LANES), F32),
            pltpu.VMEM((parent_count * SUB, LANES), F32),
            pltpu.VMEM((parent_count * SUB, LANES), F32),
            pltpu.VMEM(((parent_count + near_total + far_cap) * SUB, LANES), F32),
            pltpu.VMEM((SUB, parent_count), I32),
            pltpu.SMEM((SUB, parent_count), I32),
            pltpu.SemaphoreType.DMA((4,)),
        ],
        compiler_params=params,
        name="make_parents",
    )(children, rim, pair_order, rim_order, pair_type, new_owner, new_slot, where, weight)
    far = passed_along(far, "seg", 1)
    near = lax.all_to_all(near, "rank", split_axis=0, concat_axis=0, tiled=True)
    return pl.pallas_call(
        functools.partial(land_kernel, fields, modes),
        out_shape=jax.ShapeDtypeStruct((fields, modes, parent_count), F32),
        in_specs=[hbm, vmem, vmem],
        out_specs=vmem,
        scratch_shapes=[
            pltpu.VMEM(((parent_count + 1) * SUB, LANES), F32),
            pltpu.VMEM((SUB, near_total + LANES), I32),
            pltpu.SMEM((SUB, near_total + LANES), I32),
            pltpu.SemaphoreType.DMA((2,)),
        ],
        compiler_params=params,
        name="land_parents",
    )(home, near, far)


def solution(mesh):
    by_device = P(("seg", "rank"), None)
    in_specs = (
        P(None, None, ("seg", "rank")),
        by_device,
        by_device,
        by_device,
        P(),
        by_device,
        by_device,
    )
    out_specs = P(None, None, ("seg", "rank"))
    return jax.shard_map(
        per_device, mesh=mesh, in_specs=in_specs, out_specs=out_specs, check_vma=False
    )
```

```python
import functools

import jax
import jax.numpy as jnp
from jax import lax
from jax.experimental import pallas as pl
from jax.experimental.pallas import tpu as pltpu
from jax.sharding import PartitionSpec as P

LANES = 128
SUB = 8
F32 = jnp.float32
BF16 = jnp.bfloat16
I32 = jnp.int32
MESH = pl.DeviceIdType.MESH


def row(i):
    return pl.ds(pl.multiple_of(i * SUB, SUB), SUB)


def split(x):
    high = x.astype(BF16)
    low = (x - high.astype(F32)).astype(BF16)
    return high, low


def column_of(line):
    return jnp.broadcast_to(line, (LANES, line.shape[1])).T


def fused_kernel(
    n_seg,
    n_rank,
    near_cap,
    far_cap,
    children,
    pair_s,
    rim_s,
    kind_v,
    owner_v,
    slot_v,
    weight,
    out,
    own,
    rim,
    stage,
    ext,
    first,
    second,
    leaving,
    landed,
    final,
    sent_slots,
    got_slots,
    index_v,
    index_s,
    source_v,
    source_s,
    kind_rows,
    column_a,
    column_b,
    column_c,
    own_sem,
    rim_sems,
    slot_send,
    slot_recv,
    near_send,
    near_recv,
    index_sem,
):
    fields, modes, child_count = children.shape
    rim_len = rim_s.shape[1]
    kept = child_count - rim_len
    parent_count = child_count // 2
    kinds = weight.shape[1] // LANES
    pitch = (modes + 7) // 8 * 8
    per_group = LANES // pitch
    groups = -(-fields // per_group)
    near_total = n_rank * near_cap
    spread = (n_rank + 1) * LANES
    my_seg = lax.axis_index("seg")
    my_rank = lax.axis_index("rank")
    me = my_seg * n_rank + my_rank
    count = n_seg * n_rank
    before = (me + count - 1) % count
    after = (me + 1) % count
    seg_up = (my_seg + 1) % n_seg
    seg_down = (my_seg + n_seg - 1) % n_seg

    got_slots[...] = jnp.full_like(got_slots, parent_count)
    barrier = pltpu.get_barrier_semaphore()

    def greet(seg, rank):
        pl.semaphore_signal(barrier, inc=1, device_id=(seg, rank), device_id_type=MESH)

    greet(before // n_rank, before % n_rank)
    greet(after // n_rank, after % n_rank)
    greet(seg_up, my_rank)
    greet(seg_down, my_rank)

    def greet_rank(k, carry):
        greet(my_seg, (my_rank + k) % n_rank)
        return carry

    lax.fori_loop(1, n_rank, greet_rank, 0)
    load_own = pltpu.make_async_copy(
        children.at[:, :, pl.ds(rim_len, kept)], own, own_sem
    )
    load_own.start()
    pl.semaphore_wait(barrier, n_rank + 3)
    send_rim = pltpu.make_async_remote_copy(
        src_ref=children.at[:, :, pl.ds(0, rim_len)],
        dst_ref=rim,
        send_sem=rim_sems.at[0],
        recv_sem=rim_sems.at[1],
        device_id=(before // n_rank, before % n_rank),
        device_id_type=MESH,
    )
    send_rim.start()

    ext_flat = ext.reshape(ext.shape[0] * SUB, LANES)
    leaving_flat = leaving.reshape(leaving.shape[0] * SUB, LANES)
    landed_flat = landed.reshape(landed.shape[0] * SUB, LANES)

    owner = owner_v[...]
    slot = slot_v[...]
    owner_seg = owner // n_rank
    owner_rank = owner - owner_seg * n_rank
    distant = owner_seg != my_seg
    staying = owner == me
    bin_of = jnp.where(distant, n_rank, jnp.where(staying, -1, owner_rank))
    columns_of(bin_of, column_a)
    under = lax.broadcasted_iota(I32, (parent_count, LANES), 0)
    lane = lax.broadcasted_iota(I32, (parent_count, LANES), 1)
    for c in range(parent_count // LANES):
        at = slice(c * LANES, (c + 1) * LANES)
        same = (column_a[...] == bin_of[:, at]) & (under < lane + c * LANES)
        place = jnp.sum(jnp.where(same, 1, 0), axis=0, keepdims=True)
        stays = bin_of[:, at] < 0
        leave = jnp.where(stays, slot[:, at] + spread, bin_of[:, at] * LANES + place)
        column_b[at, :] = column_of(leave)
        info = lax.broadcasted_iota(I32, (1, LANES), 1) + c * LANES
        info = info + slot[:, at] * 1024 + kind_v[:, at] * (1024 * 1024)
        column_c[at, :] = column_of(info)

    def lines(value):
        return jnp.broadcast_to(value, (SUB, LANES))

    def invert(c):
        hit = column_b[...] == lane + c * LANES
        return jnp.max(jnp.where(hit, column_c[...], -1), axis=0, keepdims=True)

    def plan(c):
        at = pl.ds(pl.multiple_of(c * LANES, LANES), LANES)
        got = invert(c)
        used = got >= 0
        got = jnp.maximum(got, 0)
        index_v[:, at] = lines(got % 1024)
        kind_rows[:, at] = lines(got // (1024 * 1024))
        return jnp.where(used, got // 1024 % 1024, parent_count)

    def leave_plan(c, carry):
        at = pl.ds(pl.multiple_of(c * LANES, LANES), LANES)
        sent_slots[:, at] = lines(plan(c))
        return carry

    lax.fori_loop(0, n_rank + 1, leave_plan, 0)

    def slot_copy(r, seg, rank, landing):
        return pltpu.make_async_remote_copy(
            src_ref=sent_slots.at[:, pl.ds(pl.multiple_of(r * LANES, LANES), LANES)],
            dst_ref=got_slots.at[:, pl.ds(pl.multiple_of(landing * LANES, LANES), LANES)],
            send_sem=slot_send.at[r],
            recv_sem=slot_recv.at[landing],
            device_id=(seg, rank),
            device_id_type=MESH,
        )

    def near_copy(r, landing):
        size = near_cap
        return pltpu.make_async_remote_copy(
            src_ref=leaving.at[pl.ds(r * size, size)],
            dst_ref=landed.at[pl.ds(parent_count + landing * size, size)],
            send_sem=near_send.at[r],
            recv_sem=near_recv.at[landing],
            device_id=(my_seg, r),
            device_id_type=MESH,
        )

    far_copy = pltpu.make_async_remote_copy(
        src_ref=leaving.at[pl.ds(near_total, far_cap)],
        dst_ref=landed.at[pl.ds(parent_count + near_total, far_cap)],
        send_sem=near_send.at[n_rank],
        recv_sem=near_recv.at[n_rank],
        device_id=(seg_up, my_rank),
        device_id_type=MESH,
    )

    greet_slots(n_rank, my_seg, my_rank, slot_copy)
    slot_copy(n_rank, seg_up, my_rank, n_rank).start()

    def home_plan(c, carry):
        plan(n_rank + 1 + c)
        return carry

    lax.fori_loop(0, parent_count // LANES, home_plan, 0)
    to_scalar = pltpu.make_async_copy(index_v, index_s, index_sem.at[0])
    to_scalar.start()

    stage[...] = jnp.zeros_like(stage)
    load_own.wait()

    def to_rows(part, size, base):
        for g in range(groups):
            for j in range(per_group):
                f = g * per_group + j
                if f < fields:
                    stage[pitch * j : pitch * j + modes, 0:size] = part[f]

            def turn(c, carry, g=g):
                block = stage[:, pl.ds(pl.multiple_of(c * LANES, LANES), LANES)]
                ext_flat[pl.ds((base + c * LANES) * SUB + g, LANES, stride=SUB), :] = block.T
                return carry

            lax.fori_loop(0, size // LANES, turn, 0, unroll=2)

    to_rows(own, kept, 0)
    w_high, w_low = split(weight[...])
    w_both = jnp.concatenate([w_high, w_low], axis=1)
    wide = kinds * LANES
    to_scalar.wait()
    send_rim.wait()
    to_rows(rim, rim_len, child_count)

    def border(e, carry):
        ext[kept + e] = ext[child_count + rim_s[0, e]]
        return carry

    lax.fori_loop(0, rim_len, border, 0, unroll=8)

    def pick(at, base, size):
        def step(i, carry):
            q = index_s[0, at + i]
            a = pair_s[0, 2 * q]
            b = pair_s[0, 2 * q + 1]
            first[row(base + i), :] = ext[a]
            second[row(base + i), :] = ext[b]
            return carry

        lax.fori_loop(0, size, step, 0, unroll=8)

    def project(kind, size, into, base):
        parts = []
        for g in range(groups):
            at = pl.ds(g, size, stride=SUB)
            parts.append(jnp.concatenate([first[at, :], second[at, :]], axis=1))
        high, low = split(jnp.concatenate(parts, axis=0))
        both = jnp.dot(high, w_both, preferred_element_type=F32)
        total = both[:, :wide] + both[:, wide:]
        total = total + jnp.dot(low, w_high, preferred_element_type=F32)
        for g in range(groups):
            mine = total[g * size : (g + 1) * size]
            chosen = mine[:, :LANES]
            for t in range(1, kinds):
                chosen = jnp.where(kind == t, mine[:, t * LANES : (t + 1) * LANES], chosen)
            into[pl.ds(base * SUB + g, size, stride=SUB), :] = chosen

    def kind_of(c, size):
        at = pl.ds(pl.multiple_of(c * LANES, LANES), LANES)
        return column_of(kind_rows[0:1, at])[:size]

    pick(n_rank * LANES, 0, far_cap)
    project(kind_of(n_rank, far_cap), far_cap, leaving_flat, near_total)
    far_copy.start()
    together = min(LANES // near_cap, n_rank)

    def near_step(n, carry):
        kind = []
        for k in range(together):
            r = n * together + k
            pick(r * LANES, k * near_cap, near_cap)
            kind.append(kind_of(r, near_cap))
        size = together * near_cap
        project(jnp.concatenate(kind, axis=0), size, leaving_flat, n * size)
        for k in range(together):
            r = n * together + k

            @pl.when(r != my_rank)
            def _(r=r):
                near_copy(r, my_rank).start()

        return carry

    lax.fori_loop(0, n_rank // together, near_step, 0)

    def home_step(c, carry):
        pick(spread + c * LANES, 0, LANES)
        project(kind_of(n_rank + 1 + c, LANES), LANES, landed_flat, c * LANES)
        return carry

    lax.fori_loop(0, parent_count // LANES, home_step, 0)

    def slots_done(k, carry):
        r = (my_rank + k) % n_rank
        slot_copy(r, my_seg, r, r).wait()
        return carry

    lax.fori_loop(1, n_rank, slots_done, 0)
    slot_copy(n_rank, seg_up, my_rank, n_rank).wait()
    for r in range(n_rank + 1):
        size = far_cap if r == n_rank else near_cap
        tile = column_of(got_slots[0:1, r * LANES : (r + 1) * LANES])
        column_b[r * near_cap : r * near_cap + size, :] = tile[:size]
    arrivals = near_total + far_cap
    arrived = lax.broadcasted_iota(I32, (arrivals, LANES), 0) + parent_count
    slot_lane = lax.broadcasted_iota(I32, (arrivals, LANES), 1)
    for c in range(parent_count // LANES):
        hit = column_b[0:arrivals, :] == slot_lane + c * LANES
        found = jnp.max(jnp.where(hit, arrived, -1), axis=0, keepdims=True)
        own_row = c * LANES + lax.broadcasted_iota(I32, (1, LANES), 1)
        source_v[:, c * LANES : (c + 1) * LANES] = lines(
            jnp.where(found >= 0, found, own_row)
        )
    to_source = pltpu.make_async_copy(source_v, source_s, index_sem.at[1])
    to_source.start()
    to_source.wait()

    def near_done(k, carry):
        r = (my_rank + k) % n_rank
        near_copy(r, r).wait()
        return carry

    lax.fori_loop(1, n_rank, near_done, 0)
    far_copy.wait()

    def gather(s, carry):
        final[row(s), :] = landed[source_s[0, s]]
        return carry

    lax.fori_loop(0, parent_count, gather, 0, unroll=8)

    def back(c, carry):
        lanes = pl.ds(pl.multiple_of(c * LANES, LANES), LANES)
        for g in range(groups):
            tile = final[pl.ds(c * LANES * SUB + g, LANES, stride=SUB), :].T
            for j in range(per_group):
                f = g * per_group + j
                if f < fields:
                    out[f, :, lanes] = tile[pitch * j : pitch * j + modes]
        return carry

    lax.fori_loop(0, parent_count // LANES, back, 0)


def columns_of(line, ref):
    for c in range(line.shape[1] // LANES):
        at = slice(c * LANES, (c + 1) * LANES)
        ref[at, :] = column_of(line[:, at])


def greet_slots(n_rank, my_seg, my_rank, slot_copy):
    def send(k, carry):
        r = (my_rank + k) % n_rank
        slot_copy(r, my_seg, r, my_rank).start()
        return carry

    lax.fori_loop(1, n_rank, send, 0)


def wide_weights(projection):
    kinds, _, modes, _ = projection.shape
    pitch = (modes + 7) // 8 * 8
    per_group = LANES // pitch
    small = jnp.pad(projection, ((0, 0), (0, 0), (0, pitch - modes), (0, pitch - modes)))
    small = jnp.transpose(small, (1, 3, 0, 2))
    tiled = jnp.tile(small, (1, per_group, 1, per_group))
    at = jnp.arange(per_group * pitch, dtype=I32) // pitch
    tiled = jnp.where((at[:, None] == at[None, :])[None, :, None, :], tiled, 0.0)
    left = LANES - per_group * pitch
    tiled = jnp.pad(tiled, ((0, 0), (0, left), (0, 0), (0, left)))
    return tiled.reshape(2 * LANES, kinds * LANES)


def per_device(children, pair_order, rim_order, pair_type, projection, new_owner, new_slot):
    fields, modes, child_count = children.shape
    rim_len = rim_order.shape[1]
    parent_count = child_count // 2
    n_rank = lax.axis_size("rank")
    n_seg = lax.axis_size("seg")
    near_cap = parent_count // (2 * n_rank)
    far_cap = parent_count // 16
    near_total = n_rank * near_cap
    spread = (n_rank + 1) * LANES
    weight = wide_weights(projection)
    vmem = pl.BlockSpec(memory_space=pltpu.VMEM)
    smem = pl.BlockSpec(memory_space=pltpu.SMEM)
    hbm = pl.BlockSpec(memory_space=pl.ANY)
    dma = pltpu.SemaphoreType.DMA
    return pl.pallas_call(
        functools.partial(fused_kernel, n_seg, n_rank, near_cap, far_cap),
        out_shape=jax.ShapeDtypeStruct((fields, modes, parent_count), F32),
        in_specs=[hbm, smem, smem, vmem, vmem, vmem, vmem],
        out_specs=vmem,
        scratch_shapes=[
            pltpu.VMEM((fields, modes, child_count - rim_len), F32),
            pltpu.VMEM((fields, modes, rim_len), F32),
            pltpu.VMEM((LANES, child_count), F32),
            pltpu.VMEM((child_count + rim_len, SUB, LANES), F32),
            pltpu.VMEM((LANES * SUB, LANES), F32),
            pltpu.VMEM((LANES * SUB, LANES), F32),
            pltpu.VMEM((near_total + far_cap, SUB, LANES), F32),
            pltpu.VMEM((parent_count + near_total + far_cap, SUB, LANES), F32),
            pltpu.VMEM((parent_count * SUB, LANES), F32),
            pltpu.VMEM((SUB, spread), I32),
            pltpu.VMEM((SUB, spread), I32),
            pltpu.VMEM((SUB, spread + parent_count), I32),
            pltpu.SMEM((SUB, spread + parent_count), I32),
            pltpu.VMEM((SUB, parent_count), I32),
            pltpu.SMEM((SUB, parent_count), I32),
            pltpu.VMEM((SUB, spread + parent_count), I32),
            pltpu.VMEM((parent_count, LANES), I32),
            pltpu.VMEM((parent_count, LANES), I32),
            pltpu.VMEM((parent_count, LANES), I32),
            dma,
            dma((2,)),
            dma((n_rank + 1,)),
            dma((n_rank + 1,)),
            dma((n_rank + 1,)),
            dma((n_rank + 1,)),
            dma((2,)),
        ],
        compiler_params=pltpu.CompilerParams(
            vmem_limit_bytes=58 * 1024 * 1024, collective_id=0, has_side_effects=True
        ),
        name="coarsen",
    )(children, pair_order, rim_order, pair_type, new_owner, new_slot, weight)


def solution(mesh):
    by_device = P(("seg", "rank"), None)
    in_specs = (
        P(None, None, ("seg", "rank")),
        by_device,
        by_device,
        by_device,
        P(),
        by_device,
        by_device,
    )
    out_specs = P(None, None, ("seg", "rank"))
    return jax.shard_map(
        per_device, mesh=mesh, in_specs=in_specs, out_specs=out_specs, check_vma=False
    )
```

```python
import functools

import jax
import jax.numpy as jnp
from jax import lax
from jax.experimental import pallas as pl
from jax.experimental.pallas import tpu as pltpu
from jax.sharding import PartitionSpec as P

LANES = 128
SUB = 8
F32 = jnp.float32
BF16 = jnp.bfloat16
I32 = jnp.int32
MESH = pl.DeviceIdType.MESH


def row(i):
    return pl.ds(pl.multiple_of(i * SUB, SUB), SUB)


def split(x):
    high = x.astype(BF16)
    low = (x - high.astype(F32)).astype(BF16)
    return high, low


def column_of(line):
    return jnp.broadcast_to(line, (LANES, line.shape[1])).T


def fused_kernel(
    n_seg,
    n_rank,
    near_cap,
    far_cap,
    children,
    pair_s,
    rim_s,
    kind_v,
    owner_v,
    slot_v,
    projection,
    out,
    own,
    rim,
    stage,
    ext,
    first,
    second,
    leaving,
    landed,
    final,
    sent_slots,
    got_slots,
    index_v,
    index_s,
    source_v,
    source_s,
    kind_rows,
    column_a,
    column_b,
    column_c,
    weight,
    own_sem,
    rim_sems,
    slot_send,
    slot_recv,
    near_send,
    near_recv,
    index_sem,
):
    fields, modes, child_count = children.shape
    rim_len = rim_s.shape[1]
    kept = child_count - rim_len
    parent_count = child_count // 2
    kinds = projection.shape[0]
    pitch = (modes + 7) // 8 * 8
    per_group = LANES // pitch
    groups = -(-fields // per_group)
    near_total = n_rank * near_cap
    spread = (n_rank + 1) * LANES
    my_seg = lax.axis_index("seg")
    my_rank = lax.axis_index("rank")
    me = my_seg * n_rank + my_rank
    count = n_seg * n_rank
    before = (me + count - 1) % count
    after = (me + 1) % count
    seg_up = (my_seg + 1) % n_seg
    seg_down = (my_seg + n_seg - 1) % n_seg

    got_slots[...] = jnp.full_like(got_slots, parent_count)
    barrier = pltpu.get_barrier_semaphore()

    def greet(seg, rank):
        pl.semaphore_signal(barrier, inc=1, device_id=(seg, rank), device_id_type=MESH)

    greet(before // n_rank, before % n_rank)
    greet(after // n_rank, after % n_rank)
    greet(seg_up, my_rank)
    greet(seg_down, my_rank)

    def greet_rank(k, carry):
        greet(my_seg, (my_rank + k) % n_rank)
        return carry

    lax.fori_loop(1, n_rank, greet_rank, 0)
    load_own = pltpu.make_async_copy(
        children.at[:, :, pl.ds(rim_len, kept)], own, own_sem
    )
    load_own.start()
    pl.semaphore_wait(barrier, n_rank + 3)
    send_rim = pltpu.make_async_remote_copy(
        src_ref=children.at[:, :, pl.ds(0, rim_len)],
        dst_ref=rim,
        send_sem=rim_sems.at[0],
        recv_sem=rim_sems.at[1],
        device_id=(before // n_rank, before % n_rank),
        device_id_type=MESH,
    )
    send_rim.start()

    ext_flat = ext.reshape(ext.shape[0] * SUB, LANES)
    leaving_flat = leaving.reshape(leaving.shape[0] * SUB, LANES)
    landed_flat = landed.reshape(landed.shape[0] * SUB, LANES)

    owner = owner_v[...]
    slot = slot_v[...]
    owner_seg = owner // n_rank
    owner_rank = owner - owner_seg * n_rank
    distant = owner_seg != my_seg
    staying = owner == me
    bin_of = jnp.where(distant, n_rank, jnp.where(staying, -1, owner_rank))
    columns_of(bin_of, column_a)
    under = lax.broadcasted_iota(I32, (parent_count, LANES), 0)
    lane = lax.broadcasted_iota(I32, (parent_count, LANES), 1)
    for c in range(parent_count // LANES):
        at = slice(c * LANES, (c + 1) * LANES)
        same = (column_a[...] == bin_of[:, at]) & (under < lane + c * LANES)
        place = jnp.sum(jnp.where(same, 1, 0), axis=0, keepdims=True)
        stays = bin_of[:, at] < 0
        leave = jnp.where(stays, slot[:, at] + spread, bin_of[:, at] * LANES + place)
        column_b[at, :] = column_of(leave)
        info = lax.broadcasted_iota(I32, (1, LANES), 1) + c * LANES
        info = info + slot[:, at] * 1024 + kind_v[:, at] * (1024 * 1024)
        column_c[at, :] = column_of(info)

    def lines(value):
        return jnp.broadcast_to(value, (SUB, LANES))

    def invert(c):
        hit = column_b[...] == lane + c * LANES
        return jnp.max(jnp.where(hit, column_c[...], -1), axis=0, keepdims=True)

    def plan(c):
        at = pl.ds(pl.multiple_of(c * LANES, LANES), LANES)
        got = invert(c)
        used = got >= 0
        got = jnp.maximum(got, 0)
        index_v[:, at] = lines(got % 1024)
        kind_rows[:, at] = lines(got // (1024 * 1024))
        return jnp.where(used, got // 1024 % 1024, parent_count)

    def leave_plan(c, carry):
        at = pl.ds(pl.multiple_of(c * LANES, LANES), LANES)
        sent_slots[:, at] = lines(plan(c))
        return carry

    lax.fori_loop(0, n_rank + 1, leave_plan, 0)

    def slot_copy(r, seg, rank, landing):
        return pltpu.make_async_remote_copy(
            src_ref=sent_slots.at[:, pl.ds(pl.multiple_of(r * LANES, LANES), LANES)],
            dst_ref=got_slots.at[:, pl.ds(pl.multiple_of(landing * LANES, LANES), LANES)],
            send_sem=slot_send.at[r],
            recv_sem=slot_recv.at[landing],
            device_id=(seg, rank),
            device_id_type=MESH,
        )

    def near_copy(r, landing):
        size = near_cap
        return pltpu.make_async_remote_copy(
            src_ref=leaving.at[pl.ds(r * size, size), pl.ds(0, groups)],
            dst_ref=landed.at[pl.ds(parent_count + landing * size, size), pl.ds(0, groups)],
            send_sem=near_send.at[r],
            recv_sem=near_recv.at[landing],
            device_id=(my_seg, r),
            device_id_type=MESH,
        )

    far_copy = pltpu.make_async_remote_copy(
        src_ref=leaving.at[pl.ds(near_total, far_cap), pl.ds(0, groups)],
        dst_ref=landed.at[pl.ds(parent_count + near_total, far_cap), pl.ds(0, groups)],
        send_sem=near_send.at[n_rank],
        recv_sem=near_recv.at[n_rank],
        device_id=(seg_up, my_rank),
        device_id_type=MESH,
    )

    greet_slots(n_rank, my_seg, my_rank, slot_copy)
    slot_copy(n_rank, seg_up, my_rank, n_rank).start()

    def home_plan(c, carry):
        plan(n_rank + 1 + c)
        return carry

    lax.fori_loop(0, parent_count // LANES, home_plan, 0)
    to_scalar = pltpu.make_async_copy(index_v, index_s, index_sem.at[0])
    to_scalar.start()

    stage[...] = jnp.zeros_like(stage)
    load_own.wait()

    def to_rows(part, size, base):
        for g in range(groups):
            for j in range(per_group):
                f = g * per_group + j
                if f < fields:
                    stage[pitch * j : pitch * j + modes, 0:size] = part[f]

            def turn(c, carry, g=g):
                block = stage[:, pl.ds(pl.multiple_of(c * LANES, LANES), LANES)]
                ext_flat[pl.ds((base + c * LANES) * SUB + g, LANES, stride=SUB), :] = block.T
                return carry

            lax.fori_loop(0, size // LANES, turn, 0, unroll=2)

    to_rows(own, kept, 0)
    wide_at = lax.broadcasted_iota(I32, (LANES, modes), 0)
    mode_at = lax.broadcasted_iota(I32, (LANES, modes), 1)
    inside = wide_at < per_group * pitch
    spread_modes = jnp.where((wide_at % pitch == mode_at) & inside, 1.0, 0.0)
    block_a = lax.broadcasted_iota(I32, (LANES, LANES), 0) // pitch
    block_b = lax.broadcasted_iota(I32, (LANES, LANES), 1) // pitch
    for t in range(kinds):
        for child in range(2):
            tall = lax.dot_general(
                spread_modes,
                projection[t, child],
                (((1,), (1,)), ((), ())),
                precision=lax.Precision.HIGHEST,
                preferred_element_type=F32,
            )
            full = lax.dot_general(
                tall,
                spread_modes,
                (((1,), (1,)), ((), ())),
                precision=lax.Precision.HIGHEST,
                preferred_element_type=F32,
            )
            weight[child * LANES : (child + 1) * LANES, t * LANES : (t + 1) * LANES] = (
                jnp.where(block_a == block_b, full, 0.0)
            )
    w_high, w_low = split(weight[...])
    w_both = jnp.concatenate([w_high, w_low], axis=1)
    wide = kinds * LANES
    to_scalar.wait()
    send_rim.wait()
    to_rows(rim, rim_len, child_count)

    def border(e, carry):
        ext[kept + e] = ext[child_count + rim_s[0, e]]
        return carry

    lax.fori_loop(0, rim_len, border, 0, unroll=8)

    def pick(at, base, size):
        def step(i, carry):
            q = index_s[0, at + i]
            a = pair_s[0, 2 * q]
            b = pair_s[0, 2 * q + 1]
            first[row(base + i), :] = ext[a]
            second[row(base + i), :] = ext[b]
            return carry

        lax.fori_loop(0, size, step, 0, unroll=8)

    def project(kind, size, into, base):
        parts = []
        for g in range(groups):
            at = pl.ds(g, size, stride=SUB)
            parts.append(jnp.concatenate([first[at, :], second[at, :]], axis=1))
        high, low = split(jnp.concatenate(parts, axis=0))
        both = jnp.dot(high, w_both, preferred_element_type=F32)
        total = both[:, :wide] + both[:, wide:]
        total = total + jnp.dot(low, w_high, preferred_element_type=F32)
        for g in range(groups):
            mine = total[g * size : (g + 1) * size]
            chosen = mine[:, :LANES]
            for t in range(1, kinds):
                chosen = jnp.where(kind == t, mine[:, t * LANES : (t + 1) * LANES], chosen)
            into[pl.ds(base * SUB + g, size, stride=SUB), :] = chosen

    def kind_of(c, size):
        at = pl.ds(pl.multiple_of(c * LANES, LANES), LANES)
        return column_of(kind_rows[0:1, at])[:size]

    pick(n_rank * LANES, 0, far_cap)
    project(kind_of(n_rank, far_cap), far_cap, leaving_flat, near_total)
    far_copy.start()
    together = min(LANES // near_cap, n_rank)

    chunks = n_rank // together

    def near_step(k, carry):
        n = (my_rank // together + 1 + k) % chunks
        kind = []
        for k in range(together):
            r = n * together + k
            pick(r * LANES, k * near_cap, near_cap)
            kind.append(kind_of(r, near_cap))
        size = together * near_cap
        project(jnp.concatenate(kind, axis=0), size, leaving_flat, n * size)
        for k in range(together):
            r = n * together + k

            @pl.when(r != my_rank)
            def _(r=r):
                near_copy(r, my_rank).start()

        return carry

    lax.fori_loop(0, chunks, near_step, 0)

    def home_step(c, carry):
        pick(spread + c * LANES, 0, LANES)
        project(kind_of(n_rank + 1 + c, LANES), LANES, landed_flat, c * LANES)
        return carry

    lax.fori_loop(0, parent_count // LANES, home_step, 0)

    def slots_done(k, carry):
        r = (my_rank + k) % n_rank
        slot_copy(r, my_seg, r, r).wait()
        return carry

    lax.fori_loop(1, n_rank, slots_done, 0)
    slot_copy(n_rank, seg_up, my_rank, n_rank).wait()
    for r in range(n_rank + 1):
        size = far_cap if r == n_rank else near_cap
        tile = column_of(got_slots[0:1, r * LANES : (r + 1) * LANES])
        column_b[r * near_cap : r * near_cap + size, :] = tile[:size]
    arrivals = near_total + far_cap
    arrived = lax.broadcasted_iota(I32, (arrivals, LANES), 0) + parent_count
    slot_lane = lax.broadcasted_iota(I32, (arrivals, LANES), 1)
    for c in range(parent_count // LANES):
        hit = column_b[0:arrivals, :] == slot_lane + c * LANES
        found = jnp.max(jnp.where(hit, arrived, -1), axis=0, keepdims=True)
        own_row = c * LANES + lax.broadcasted_iota(I32, (1, LANES), 1)
        source_v[:, c * LANES : (c + 1) * LANES] = lines(
            jnp.where(found >= 0, found, own_row)
        )
    to_source = pltpu.make_async_copy(source_v, source_s, index_sem.at[1])
    to_source.start()
    to_source.wait()

    def near_done(k, carry):
        r = (my_rank + k) % n_rank
        near_copy(r, r).wait()
        return carry

    lax.fori_loop(1, n_rank, near_done, 0)
    far_copy.wait()

    def gather(s, carry):
        final[row(s), :] = landed[source_s[0, s]]
        return carry

    lax.fori_loop(0, parent_count, gather, 0, unroll=8)

    def back(c, carry):
        lanes = pl.ds(pl.multiple_of(c * LANES, LANES), LANES)
        for g in range(groups):
            tile = final[pl.ds(c * LANES * SUB + g, LANES, stride=SUB), :].T
            for j in range(per_group):
                f = g * per_group + j
                if f < fields:
                    out[f, :, lanes] = tile[pitch * j : pitch * j + modes]
        return carry

    lax.fori_loop(0, parent_count // LANES, back, 0)


def columns_of(line, ref):
    for c in range(line.shape[1] // LANES):
        at = slice(c * LANES, (c + 1) * LANES)
        ref[at, :] = column_of(line[:, at])


def greet_slots(n_rank, my_seg, my_rank, slot_copy):
    def send(k, carry):
        r = (my_rank + k) % n_rank
        slot_copy(r, my_seg, r, my_rank).start()
        return carry

    lax.fori_loop(1, n_rank, send, 0)


def per_device(children, pair_order, rim_order, pair_type, projection, new_owner, new_slot):
    fields, modes, child_count = children.shape
    rim_len = rim_order.shape[1]
    parent_count = child_count // 2
    n_rank = lax.axis_size("rank")
    n_seg = lax.axis_size("seg")
    near_cap = parent_count // (2 * n_rank)
    far_cap = parent_count // 16
    near_total = n_rank * near_cap
    spread = (n_rank + 1) * LANES
    kinds = projection.shape[0]
    vmem = pl.BlockSpec(memory_space=pltpu.VMEM)
    smem = pl.BlockSpec(memory_space=pltpu.SMEM)
    hbm = pl.BlockSpec(memory_space=pl.ANY)
    dma = pltpu.SemaphoreType.DMA
    return pl.pallas_call(
        functools.partial(fused_kernel, n_seg, n_rank, near_cap, far_cap),
        out_shape=jax.ShapeDtypeStruct((fields, modes, parent_count), F32),
        in_specs=[hbm, smem, smem, vmem, vmem, vmem, vmem],
        out_specs=vmem,
        scratch_shapes=[
            pltpu.VMEM((fields, modes, child_count - rim_len), F32),
            pltpu.VMEM((fields, modes, rim_len), F32),
            pltpu.VMEM((LANES, child_count), F32),
            pltpu.VMEM((child_count + rim_len, SUB, LANES), F32),
            pltpu.VMEM((LANES * SUB, LANES), F32),
            pltpu.VMEM((LANES * SUB, LANES), F32),
            pltpu.VMEM((near_total + far_cap, SUB, LANES), F32),
            pltpu.VMEM((parent_count + near_total + far_cap, SUB, LANES), F32),
            pltpu.VMEM((parent_count * SUB, LANES), F32),
            pltpu.VMEM((SUB, spread), I32),
            pltpu.VMEM((SUB, spread), I32),
            pltpu.VMEM((SUB, spread + parent_count), I32),
            pltpu.SMEM((SUB, spread + parent_count), I32),
            pltpu.VMEM((SUB, parent_count), I32),
            pltpu.SMEM((SUB, parent_count), I32),
            pltpu.VMEM((SUB, spread + parent_count), I32),
            pltpu.VMEM((parent_count, LANES), I32),
            pltpu.VMEM((parent_count, LANES), I32),
            pltpu.VMEM((parent_count, LANES), I32),
            pltpu.VMEM((2 * LANES, kinds * LANES), F32),
            dma,
            dma((2,)),
            dma((n_rank + 1,)),
            dma((n_rank + 1,)),
            dma((n_rank + 1,)),
            dma((n_rank + 1,)),
            dma((2,)),
        ],
        compiler_params=pltpu.CompilerParams(
            vmem_limit_bytes=58 * 1024 * 1024, collective_id=0, has_side_effects=True
        ),
        name="coarsen",
    )(children, pair_order, rim_order, pair_type, new_owner, new_slot, projection)


def solution(mesh):
    by_device = P(("seg", "rank"), None)
    in_specs = (
        P(None, None, ("seg", "rank")),
        by_device,
        by_device,
        by_device,
        P(),
        by_device,
        by_device,
    )
    out_specs = P(None, None, ("seg", "rank"))
    return jax.shard_map(
        per_device, mesh=mesh, in_specs=in_specs, out_specs=out_specs, check_vma=False
    )
```

```python
import functools

import jax
import jax.numpy as jnp
from jax import lax
from jax.experimental import pallas as pl
from jax.experimental.pallas import tpu as pltpu
from jax.sharding import PartitionSpec as P

LANES = 128
SUB = 8
F32 = jnp.float32
BF16 = jnp.bfloat16
I32 = jnp.int32
MESH = pl.DeviceIdType.MESH


def row(i):
    return pl.ds(pl.multiple_of(i * SUB, SUB), SUB)


def split(x):
    high = x.astype(BF16)
    low = (x - high.astype(F32)).astype(BF16)
    return high, low


def column_of(line):
    return jnp.broadcast_to(line, (LANES, line.shape[1])).T


def fused_kernel(
    n_seg,
    n_rank,
    near_cap,
    far_cap,
    children,
    pair_s,
    rim_s,
    kind_v,
    owner_v,
    slot_v,
    projection,
    out,
    own,
    rim,
    stage,
    ext,
    first,
    second,
    leaving,
    landed,
    final,
    sent_slots,
    got_slots,
    index_v,
    index_s,
    source_v,
    source_s,
    kind_rows,
    column_a,
    column_b,
    column_c,
    weight,
    own_sem,
    rim_sems,
    slot_send,
    slot_recv,
    near_send,
    near_recv,
    index_sem,
):
    fields, modes, child_count = children.shape
    rim_len = rim_s.shape[1]
    kept = child_count - rim_len
    parent_count = child_count // 2
    kinds = projection.shape[0]
    pitch = (modes + 7) // 8 * 8
    per_group = LANES // pitch
    groups = -(-fields // per_group)
    near_total = n_rank * near_cap
    spread = (n_rank + 1) * LANES
    my_seg = lax.axis_index("seg")
    my_rank = lax.axis_index("rank")
    me = my_seg * n_rank + my_rank
    count = n_seg * n_rank
    before = (me + count - 1) % count
    after = (me + 1) % count
    seg_up = (my_seg + 1) % n_seg
    seg_down = (my_seg + n_seg - 1) % n_seg

    got_slots[...] = jnp.full_like(got_slots, parent_count)
    barrier = pltpu.get_barrier_semaphore()

    def greet(seg, rank):
        pl.semaphore_signal(barrier, inc=1, device_id=(seg, rank), device_id_type=MESH)

    greet(before // n_rank, before % n_rank)
    greet(after // n_rank, after % n_rank)
    greet(seg_up, my_rank)
    greet(seg_down, my_rank)

    def greet_rank(k, carry):
        greet(my_seg, (my_rank + k) % n_rank)
        return carry

    lax.fori_loop(1, n_rank, greet_rank, 0)
    load_own = pltpu.make_async_copy(
        children.at[:, :, pl.ds(rim_len, kept)], own, own_sem
    )
    load_own.start()
    pl.semaphore_wait(barrier, n_rank + 3)
    send_rim = pltpu.make_async_remote_copy(
        src_ref=children.at[:, :, pl.ds(0, rim_len)],
        dst_ref=rim,
        send_sem=rim_sems.at[0],
        recv_sem=rim_sems.at[1],
        device_id=(before // n_rank, before % n_rank),
        device_id_type=MESH,
    )
    send_rim.start()

    ext_flat = ext.reshape(ext.shape[0] * SUB, LANES)
    leaving_flat = leaving.reshape(leaving.shape[0] * SUB, LANES)
    landed_flat = landed.reshape(landed.shape[0] * SUB, LANES)

    owner = owner_v[...]
    slot = slot_v[...]
    owner_seg = owner // n_rank
    owner_rank = owner - owner_seg * n_rank
    distant = owner_seg != my_seg
    staying = owner == me
    bin_of = jnp.where(distant, n_rank, jnp.where(staying, -1, owner_rank))
    columns_of(bin_of, column_a)
    under = lax.broadcasted_iota(I32, (parent_count, LANES), 0)
    lane = lax.broadcasted_iota(I32, (parent_count, LANES), 1)
    for c in range(parent_count // LANES):
        at = slice(c * LANES, (c + 1) * LANES)
        same = (column_a[...] == bin_of[:, at]) & (under < lane + c * LANES)
        place = jnp.sum(jnp.where(same, 1, 0), axis=0, keepdims=True)
        stays = bin_of[:, at] < 0
        leave = jnp.where(stays, slot[:, at] + spread, bin_of[:, at] * LANES + place)
        column_b[at, :] = column_of(leave)
        info = lax.broadcasted_iota(I32, (1, LANES), 1) + c * LANES
        info = info + slot[:, at] * 1024 + kind_v[:, at] * (1024 * 1024)
        column_c[at, :] = column_of(info)

    def lines(value):
        return jnp.broadcast_to(value, (SUB, LANES))

    def invert(c):
        hit = column_b[...] == lane + c * LANES
        return jnp.max(jnp.where(hit, column_c[...], -1), axis=0, keepdims=True)

    def plan(c):
        at = pl.ds(pl.multiple_of(c * LANES, LANES), LANES)
        got = invert(c)
        used = got >= 0
        got = jnp.maximum(got, 0)
        index_v[:, at] = lines(got % 1024)
        kind_rows[:, at] = lines(got // (1024 * 1024))
        return jnp.where(used, got // 1024 % 1024, parent_count)

    def leave_plan(c, carry):
        at = pl.ds(pl.multiple_of(c * LANES, LANES), LANES)
        sent_slots[:, at] = lines(plan(c))
        return carry

    lax.fori_loop(0, n_rank + 1, leave_plan, 0)

    def slot_copy(r, seg, rank, landing):
        return pltpu.make_async_remote_copy(
            src_ref=sent_slots.at[:, pl.ds(pl.multiple_of(r * LANES, LANES), LANES)],
            dst_ref=got_slots.at[:, pl.ds(pl.multiple_of(landing * LANES, LANES), LANES)],
            send_sem=slot_send.at[r],
            recv_sem=slot_recv.at[landing],
            device_id=(seg, rank),
            device_id_type=MESH,
        )

    def near_copy(r, landing):
        size = near_cap
        return pltpu.make_async_remote_copy(
            src_ref=leaving.at[pl.ds(r * size, size), pl.ds(0, groups)],
            dst_ref=landed.at[pl.ds(parent_count + landing * size, size), pl.ds(0, groups)],
            send_sem=near_send.at[r],
            recv_sem=near_recv.at[landing],
            device_id=(my_seg, r),
            device_id_type=MESH,
        )

    far_copy = pltpu.make_async_remote_copy(
        src_ref=leaving.at[pl.ds(near_total, far_cap), pl.ds(0, groups)],
        dst_ref=landed.at[pl.ds(parent_count + near_total, far_cap), pl.ds(0, groups)],
        send_sem=near_send.at[n_rank],
        recv_sem=near_recv.at[n_rank],
        device_id=(seg_up, my_rank),
        device_id_type=MESH,
    )

    greet_slots(n_rank, my_seg, my_rank, slot_copy)
    slot_copy(n_rank, seg_up, my_rank, n_rank).start()

    def home_plan(c, carry):
        plan(n_rank + 1 + c)
        return carry

    lax.fori_loop(0, parent_count // LANES, home_plan, 0)
    to_scalar = pltpu.make_async_copy(index_v, index_s, index_sem.at[0])
    to_scalar.start()

    stage[...] = jnp.zeros_like(stage)
    load_own.wait()

    def to_rows(part, size, base):
        for g in range(groups):
            for j in range(per_group):
                f = g * per_group + j
                if f < fields:
                    stage[pitch * j : pitch * j + modes, 0:size] = part[f]

            def turn(c, carry, g=g):
                block = stage[:, pl.ds(pl.multiple_of(c * LANES, LANES), LANES)]
                ext_flat[pl.ds((base + c * LANES) * SUB + g, LANES, stride=SUB), :] = block.T
                return carry

            lax.fori_loop(0, size // LANES, turn, 0, unroll=min(7, size // LANES))

    to_rows(own, kept, 0)
    wide_at = lax.broadcasted_iota(I32, (LANES, modes), 0)
    mode_at = lax.broadcasted_iota(I32, (LANES, modes), 1)
    inside = wide_at < per_group * pitch
    spread_modes = jnp.where((wide_at % pitch == mode_at) & inside, 1.0, 0.0)
    block_a = lax.broadcasted_iota(I32, (LANES, LANES), 0) // pitch
    block_b = lax.broadcasted_iota(I32, (LANES, LANES), 1) // pitch
    for t in range(kinds):
        for child in range(2):
            tall = lax.dot_general(
                spread_modes,
                projection[t, child],
                (((1,), (1,)), ((), ())),
                precision=lax.Precision.HIGHEST,
                preferred_element_type=F32,
            )
            full = lax.dot_general(
                tall,
                spread_modes,
                (((1,), (1,)), ((), ())),
                precision=lax.Precision.HIGHEST,
                preferred_element_type=F32,
            )
            weight[child * LANES : (child + 1) * LANES, t * LANES : (t + 1) * LANES] = (
                jnp.where(block_a == block_b, full, 0.0)
            )
    w_high, w_low = split(weight[...])
    w_both = jnp.concatenate([w_high, w_low], axis=1)
    wide = kinds * LANES
    to_scalar.wait()
    send_rim.wait()
    to_rows(rim, rim_len, child_count)

    def border(e, carry):
        ext[kept + e] = ext[child_count + rim_s[0, e]]
        return carry

    lax.fori_loop(0, rim_len, border, 0, unroll=8)

    def pick(at, base, size):
        def step(i, carry):
            q = index_s[0, at + i]
            a = pair_s[0, 2 * q]
            b = pair_s[0, 2 * q + 1]
            first[row(base + i), :] = ext[a]
            second[row(base + i), :] = ext[b]
            return carry

        lax.fori_loop(0, size, step, 0, unroll=16)

    def project(kind, size, into, base):
        parts = []
        for g in range(groups):
            at = pl.ds(g, size, stride=SUB)
            parts.append(jnp.concatenate([first[at, :], second[at, :]], axis=1))
        high, low = split(jnp.concatenate(parts, axis=0))
        both = jnp.dot(high, w_both, preferred_element_type=F32)
        total = both[:, :wide] + both[:, wide:]
        total = total + jnp.dot(low, w_high, preferred_element_type=F32)
        for g in range(groups):
            mine = total[g * size : (g + 1) * size]
            chosen = mine[:, :LANES]
            for t in range(1, kinds):
                chosen = jnp.where(kind == t, mine[:, t * LANES : (t + 1) * LANES], chosen)
            into[pl.ds(base * SUB + g, size, stride=SUB), :] = chosen

    def kind_of(c, size):
        at = pl.ds(pl.multiple_of(c * LANES, LANES), LANES)
        return column_of(kind_rows[0:1, at])[:size]

    pick(n_rank * LANES, 0, far_cap)
    project(kind_of(n_rank, far_cap), far_cap, leaving_flat, near_total)
    far_copy.start()
    together = min(LANES // near_cap, n_rank)

    chunks = n_rank // together

    def near_step(k, carry):
        n = (my_rank // together + 1 + k) % chunks
        kind = []
        for k in range(together):
            r = n * together + k
            pick(r * LANES, k * near_cap, near_cap)
            kind.append(kind_of(r, near_cap))
        size = together * near_cap
        project(jnp.concatenate(kind, axis=0), size, leaving_flat, n * size)
        for k in range(together):
            r = n * together + k

            @pl.when(r != my_rank)
            def _(r=r):
                near_copy(r, my_rank).start()

        return carry

    lax.fori_loop(0, chunks, near_step, 0)

    def home_step(c, carry):
        pick(spread + c * LANES, 0, LANES)
        project(kind_of(n_rank + 1 + c, LANES), LANES, landed_flat, c * LANES)
        return carry

    lax.fori_loop(0, parent_count // LANES, home_step, 0)

    def slots_done(k, carry):
        r = (my_rank + k) % n_rank
        slot_copy(r, my_seg, r, r).wait()
        return carry

    lax.fori_loop(1, n_rank, slots_done, 0)
    slot_copy(n_rank, seg_up, my_rank, n_rank).wait()
    for r in range(n_rank + 1):
        size = far_cap if r == n_rank else near_cap
        tile = column_of(got_slots[0:1, r * LANES : (r + 1) * LANES])
        column_b[r * near_cap : r * near_cap + size, :] = tile[:size]
    arrivals = near_total + far_cap
    arrived = lax.broadcasted_iota(I32, (arrivals, LANES), 0) + parent_count
    slot_lane = lax.broadcasted_iota(I32, (arrivals, LANES), 1)
    for c in range(parent_count // LANES):
        hit = column_b[0:arrivals, :] == slot_lane + c * LANES
        found = jnp.max(jnp.where(hit, arrived, -1), axis=0, keepdims=True)
        own_row = c * LANES + lax.broadcasted_iota(I32, (1, LANES), 1)
        source_v[:, c * LANES : (c + 1) * LANES] = lines(
            jnp.where(found >= 0, found, own_row)
        )
    to_source = pltpu.make_async_copy(source_v, source_s, index_sem.at[1])
    to_source.start()
    to_source.wait()

    def near_done(k, carry):
        r = (my_rank + k) % n_rank
        near_copy(r, r).wait()
        return carry

    lax.fori_loop(1, n_rank, near_done, 0)
    far_copy.wait()

    def gather(s, carry):
        final[row(s), :] = landed[source_s[0, s]]
        return carry

    lax.fori_loop(0, parent_count, gather, 0, unroll=16)

    def back(c, carry):
        lanes = pl.ds(pl.multiple_of(c * LANES, LANES), LANES)
        for g in range(groups):
            tile = final[pl.ds(c * LANES * SUB + g, LANES, stride=SUB), :].T
            for j in range(per_group):
                f = g * per_group + j
                if f < fields:
                    out[f, :, lanes] = tile[pitch * j : pitch * j + modes]
        return carry

    lax.fori_loop(0, parent_count // LANES, back, 0)


def columns_of(line, ref):
    for c in range(line.shape[1] // LANES):
        at = slice(c * LANES, (c + 1) * LANES)
        ref[at, :] = column_of(line[:, at])


def greet_slots(n_rank, my_seg, my_rank, slot_copy):
    def send(k, carry):
        r = (my_rank + k) % n_rank
        slot_copy(r, my_seg, r, my_rank).start()
        return carry

    lax.fori_loop(1, n_rank, send, 0)


def per_device(children, pair_order, rim_order, pair_type, projection, new_owner, new_slot):
    fields, modes, child_count = children.shape
    rim_len = rim_order.shape[1]
    parent_count = child_count // 2
    n_rank = lax.axis_size("rank")
    n_seg = lax.axis_size("seg")
    near_cap = parent_count // (2 * n_rank)
    far_cap = parent_count // 16
    near_total = n_rank * near_cap
    spread = (n_rank + 1) * LANES
    kinds = projection.shape[0]
    vmem = pl.BlockSpec(memory_space=pltpu.VMEM)
    smem = pl.BlockSpec(memory_space=pltpu.SMEM)
    hbm = pl.BlockSpec(memory_space=pl.ANY)
    dma = pltpu.SemaphoreType.DMA
    return pl.pallas_call(
        functools.partial(fused_kernel, n_seg, n_rank, near_cap, far_cap),
        out_shape=jax.ShapeDtypeStruct((fields, modes, parent_count), F32),
        in_specs=[hbm, smem, smem, vmem, vmem, vmem, vmem],
        out_specs=vmem,
        scratch_shapes=[
            pltpu.VMEM((fields, modes, child_count - rim_len), F32),
            pltpu.VMEM((fields, modes, rim_len), F32),
            pltpu.VMEM((LANES, child_count), F32),
            pltpu.VMEM((child_count + rim_len, SUB, LANES), F32),
            pltpu.VMEM((LANES * SUB, LANES), F32),
            pltpu.VMEM((LANES * SUB, LANES), F32),
            pltpu.VMEM((near_total + far_cap, SUB, LANES), F32),
            pltpu.VMEM((parent_count + near_total + far_cap, SUB, LANES), F32),
            pltpu.VMEM((parent_count * SUB, LANES), F32),
            pltpu.VMEM((SUB, spread), I32),
            pltpu.VMEM((SUB, spread), I32),
            pltpu.VMEM((SUB, spread + parent_count), I32),
            pltpu.SMEM((SUB, spread + parent_count), I32),
            pltpu.VMEM((SUB, parent_count), I32),
            pltpu.SMEM((SUB, parent_count), I32),
            pltpu.VMEM((SUB, spread + parent_count), I32),
            pltpu.VMEM((parent_count, LANES), I32),
            pltpu.VMEM((parent_count, LANES), I32),
            pltpu.VMEM((parent_count, LANES), I32),
            pltpu.VMEM((2 * LANES, kinds * LANES), F32),
            dma,
            dma((2,)),
            dma((n_rank + 1,)),
            dma((n_rank + 1,)),
            dma((n_rank + 1,)),
            dma((n_rank + 1,)),
            dma((2,)),
        ],
        compiler_params=pltpu.CompilerParams(
            vmem_limit_bytes=58 * 1024 * 1024, collective_id=0, has_side_effects=True
        ),
        name="coarsen",
    )(children, pair_order, rim_order, pair_type, new_owner, new_slot, projection)


def solution(mesh):
    by_device = P(("seg", "rank"), None)
    in_specs = (
        P(None, None, ("seg", "rank")),
        by_device,
        by_device,
        by_device,
        P(),
        by_device,
        by_device,
    )
    out_specs = P(None, None, ("seg", "rank"))
    return jax.shard_map(
        per_device, mesh=mesh, in_specs=in_specs, out_specs=out_specs, check_vma=False
    )
```
